512 devices in a mesh: dp: 4 (over x), ctx: 32 (over z, core), ch: 4 (over y).
Axes of the slice: x: 4, y: 4, z: 16, core: 2. Of those that a mesh axis runs over, the one named last changes fastest.
Arguments:
- gate_input: bfloat16 [4, 4096, 4096], P('dp', 'ctx', 'ch'), may hold values from -6 to 6
- conv_input: bfloat16 [4, 4096, 4096], P('dp', 'ctx', 'ch'), may hold values from -6 to 6
- grad_output: bfloat16 [4, 4096, 4096], P('dp', 'ctx', 'ch'), may hold values from -6 to 6
- kernel: bfloat16 [128, 640], P('ch'), may hold values from -0.25 to 0.25
Outputs:
- output: bfloat16 [4, 4096, 4096], P('dp', 'ctx', 'ch')
- grad_gate: bfloat16 [4, 4096, 4096], P('dp', 'ctx', 'ch')
- grad_conv: bfloat16 [4, 4096, 4096], P('dp', 'ctx', 'ch')
- grad_kernel: float32 [128, 640], P('ch', ('dp', 'ctx'))
The draws below stay inside these ranges and needn't reach their ends.
All inputs are finite; a program needn't handle non-finite values.
Results may differ from the reference program's by a relative error of at most 0.0049.
Values may be sent and summed in bfloat16 or wider, within the bound.
No kernel may reach another device: no remote copies, remote signals or barrier semaphores. Data moves between devices by JAX's collectives and lax.ppermute only.
A program may use at most 64 MiB of HBM per device.

```python
import math
import jax
import jax.numpy as jnp
from jax import lax

D = 4096
GROUP = 32
FG = 128
TOK_DEV = 128
LAG_BLOCKS = 5
LAGS = 640
SEQ = 4096
SEQS = 4
N_CTX = 32


def shard_levels(key, shape, split, least, high):
    def one(dim, parts):
        heights = jax.random.uniform(jax.random.fold_in(jax.random.fold_in(key, 6), dim), (parts,), jnp.float32, least / len(split), high / len(split))
        return jnp.repeat(jnp.exp(heights), shape[dim] // parts).reshape((-1,) + (1,) * (len(shape) - dim - 1))

    loudness = one(*split[0])
    for cut in split[1:]:
        loudness = loudness * one(*cut)
    return loudness


def normal_values(key, shape, deviation, bound, pieces=(), kind=jnp.bfloat16):
    values = jax.random.normal(key, shape, jnp.float32) * deviation
    if len(pieces) > 0:
        values = shard_levels(key, shape, pieces, -0.22, 0.18) * values
    return jnp.clip(values, min=-bound, max=bound).astype(kind)


def setup_inputs(seed: int = 0) -> dict:
    keys = jax.random.split(jax.random.key(seed), 5)
    gate_input = normal_values(keys[0], (SEQS, SEQ, D), 1.0, 6.0, ((0, 4), (1, 32), (2, 4)))
    conv_input = normal_values(keys[1], (SEQS, SEQ, D), 1.0, 6.0, ((0, 4), (1, 32), (2, 4)))
    grad_output = normal_values(keys[2], (SEQS, SEQ, D), 1.0, 6.0, ((0, 4), (1, 32), (2, 4)))
    kernel = normal_values(keys[3], (FG, LAGS), LAGS ** -0.5, 0.25, ((0, 4),))
    return dict(gate_input=gate_input, conv_input=conv_input, grad_output=grad_output, kernel=kernel)


def toeplitz(kernel, offset):
    positions = jnp.arange(TOK_DEV, dtype=jnp.int32)
    indices = offset.astype(jnp.int32) * TOK_DEV + positions[:, None] - positions[None, :]
    lagged = jnp.take(kernel, jnp.clip(indices, 0, LAGS - 1), axis=1)
    valid = (indices >= 0) & (indices < LAGS)
    return jnp.where(valid[None], lagged, jnp.zeros_like(lagged))

def diagonal_sums(matrix):
    groups = matrix.shape[0]
    extent = matrix.shape[1]
    flipped = matrix[:, :, ::-1]
    padded = jnp.pad(flipped, ((0, 0), (0, 0), (0, extent)))
    flattened = padded.reshape(groups, 2 * extent * extent)[:, :extent * (2 * extent - 1)]
    totals = lax.optimization_barrier(jnp.sum(flattened.reshape(groups, extent, 2 * extent - 1).astype(jnp.float32), axis=1))
    return jnp.pad(totals, ((0, 0), (0, 1)))

def reference(gate_input, conv_input, grad_output, kernel):

    def forward_block(offset, block):
        matrix = toeplitz(kernel, offset).astype(jnp.float32)
        shaped = block.astype(jnp.float32).reshape(TOK_DEV, FG, GROUP)
        return jnp.einsum('gab,bgc->agc', matrix, shaped).reshape(TOK_DEV, D)

    def backward_block(offset, block):
        matrix = toeplitz(kernel, offset).astype(jnp.float32)
        shaped = block.astype(jnp.float32).reshape(TOK_DEV, FG, GROUP)
        return jnp.einsum('gab,agc->bgc', matrix, shaped).reshape(TOK_DEV, D)

    def pair_block(grad_block, value_block):
        left_side = grad_block.astype(jnp.float32).reshape(TOK_DEV, FG, GROUP)
        right_side = value_block.astype(jnp.float32).reshape(TOK_DEV, FG, GROUP)
        return jnp.einsum('agc,bgc->gab', left_side, right_side).astype(jnp.bfloat16)
    block_ids = jnp.arange(N_CTX, dtype=jnp.int32)
    offset_ids = jnp.arange(LAG_BLOCKS + 1, dtype=jnp.int32)

    def one_sample(inputs):
        gate_rows, value_rows, grad_rows = inputs
        value_blocks = value_rows.reshape(N_CTX, TOK_DEV, D)

        def forward_row(target):

            def add_term(source, running):
                return running + forward_block(target - source, value_blocks[source])
            first = jnp.maximum(target - LAG_BLOCKS, 0).astype(jnp.int32)
            return lax.fori_loop(first, target + 1, add_term, jnp.zeros((TOK_DEV, D), jnp.float32))
        convolved = lax.map(forward_row, block_ids).reshape(SEQ, D)
        output = (gate_rows.astype(jnp.float32) * convolved).astype(jnp.bfloat16)
        grad_mixed = (gate_rows.astype(jnp.float32) * grad_rows.astype(jnp.float32)).astype(jnp.bfloat16)
        grad_gate = (grad_rows.astype(jnp.float32) * convolved).astype(jnp.bfloat16)
        grad_blocks = grad_mixed.reshape(N_CTX, TOK_DEV, D)

        def backward_row(source):

            def add_term(target, running):
                return running + backward_block(target - source, grad_blocks[target])
            last = jnp.minimum(source + LAG_BLOCKS + 1, N_CTX).astype(jnp.int32)
            return lax.fori_loop(source, last, add_term, jnp.zeros((TOK_DEV, D), jnp.float32))
        grad_conv = lax.map(backward_row, block_ids).reshape(SEQ, D).astype(jnp.bfloat16)

        def lag_window(offset):

            def add_pair(target, running):
                return running + pair_block(grad_blocks[target], value_blocks[target - offset]).astype(jnp.float32)
            summed = lax.fori_loop(offset, jnp.int32(N_CTX), add_pair, jnp.zeros((FG, TOK_DEV, TOK_DEV), jnp.float32))
            return diagonal_sums(summed)
        windows = lax.map(lag_window, offset_ids)
        return (output, grad_gate, grad_conv, windows)
    output, grad_gate, grad_conv, windows = lax.map(one_sample, (gate_input, conv_input, grad_output))
    windows = lax.optimization_barrier(jnp.sum(windows, axis=0))
    first_half = windows[:, :, :TOK_DEV]
    second_half = windows[:, :, TOK_DEV:]
    zero_block = jnp.zeros((1, FG, TOK_DEV), jnp.float32)
    stacked = jnp.concatenate([first_half, zero_block], axis=0) + jnp.concatenate([zero_block, second_half], axis=0)
    buffer = jnp.transpose(stacked, (1, 0, 2)).reshape(FG, (LAG_BLOCKS + 2) * TOK_DEV)
    grad_kernel = buffer[:, TOK_DEV - 1:TOK_DEV - 1 + LAGS] / math.sqrt(SEQS * SEQ)
    return (output, grad_gate, grad_conv, grad_kernel)
```

```python
import math

import jax
import jax.numpy as jnp
from jax import lax
from jax.experimental import pallas as pl
from jax.experimental.pallas import tpu as pltpu
from jax.sharding import PartitionSpec as P

LANES = 128


def passed_along(x, axis, by):
    length = lax.axis_size(axis)
    pairs = [(i, i + by) for i in range(length) if 0 <= i + by < length]
    return lax.ppermute(x, axis, pairs)


def exchange_matrix(size):
    rows = lax.broadcasted_iota(jnp.int32, (size, size), 0)
    cols = lax.broadcasted_iota(jnp.int32, (size, size), 1)
    return jnp.where(rows + cols == size - 1, 1.0, 0.0).astype(jnp.bfloat16)


def reversed_rows(flip, block):
    return jnp.dot(flip, block, preferred_element_type=jnp.float32).astype(jnp.bfloat16)


def prepare_kernel(gate_ref, value_ref, grad_ref, mixed_ref, reversed_ref):
    flip = exchange_matrix(value_ref.shape[0])
    mixed_ref[...] = (
        gate_ref[...].astype(jnp.float32) * grad_ref[...].astype(jnp.float32)
    ).astype(jnp.bfloat16)
    reversed_ref[...] = reversed_rows(flip, value_ref[...])


def prepare(gate_rows, value_rows, grad_rows):
    shape = jax.ShapeDtypeStruct(gate_rows.shape, jnp.bfloat16)
    return pl.pallas_call(
        prepare_kernel,
        out_shape=(shape, shape),
        name="prepare",
        cost_estimate=pl.CostEstimate(flops=40_000_000, bytes_accessed=1_400_000, transcendentals=0),
    )(gate_rows, value_rows, grad_rows)


def toeplitz_kernel(taps_ref, matrix_ref):
    groups, tok_rows, width = matrix_ref.shape
    taps = taps_ref[...].astype(jnp.float32)
    padded = jnp.concatenate([taps, jnp.zeros((groups, width - taps.shape[1]), jnp.float32)], axis=1)
    for g in range(groups):
        spread = jnp.broadcast_to(padded[g : g + 1, :], (tok_rows, width))
        sheared = pltpu.roll(spread, 0, 1, stride=1, stride_axis=0)
        matrix_ref[g] = sheared.astype(jnp.bfloat16)


def toeplitz(taps, tok_rows):
    groups, lag_count = taps.shape
    step = 8
    width = lag_count + tok_rows
    return pl.pallas_call(
        toeplitz_kernel,
        grid=(groups // step,),
        in_specs=[pl.BlockSpec((step, lag_count), lambda i: (i, 0))],
        out_specs=pl.BlockSpec((step, tok_rows, width), lambda i: (i, 0, 0)),
        out_shape=jax.ShapeDtypeStruct((groups, tok_rows, width), jnp.bfloat16),
        name="toeplitz",
        cost_estimate=pl.CostEstimate(flops=12_000_000_000, bytes_accessed=6_400_000, transcendentals=0),
    )(taps)


def lane_group(shape, group_size):
    return lax.broadcasted_iota(jnp.int32, shape, len(shape) - 1) // group_size


def pair_kernel(group_size, lag_count, *refs):
    *block_refs, out_ref = refs
    spans = len(block_refs) // 3
    tok_rows = block_refs[0].shape[0]
    per_chunk = LANES // group_size
    owner = lane_group((tok_rows, LANES), group_size)
    width = 3 * tok_rows
    sums = [[None] * (2 * spans + 1) for _ in range(per_chunk)]
    for k in range(spans):
        grad = block_refs[3 * k][...]
        right = jnp.concatenate([block_refs[3 * k + 1][...], block_refs[3 * k + 2][...]], axis=0)
        left = jnp.concatenate(
            [jnp.where(owner == g, grad, jnp.zeros_like(grad)) for g in range(per_chunk)], axis=0
        )
        paired = lax.dot_general(
            left, right, (((1,), (1,)), ((), ())), preferred_element_type=jnp.float32
        )
        for g in range(per_chunk):
            mine = paired[g * tok_rows : (g + 1) * tok_rows]
            wide = jnp.concatenate([mine, jnp.zeros((tok_rows, tok_rows), jnp.float32)], axis=1)
            sheared = pltpu.roll(wide, 1, 1, stride=1, stride_axis=0)
            total = jnp.sum(sheared, axis=0, keepdims=True)
            for part in range(3):
                piece = total[:, part * tok_rows : (part + 1) * tok_rows]
                held = sums[g][2 * k + part]
                sums[g][2 * k + part] = piece if held is None else held + piece
    lag_blocks = lag_count // tok_rows
    for g in range(per_chunk):
        out_ref[0, g : g + 1, :] = jnp.concatenate(sums[g][1 : 1 + lag_blocks], axis=1)


def pair_sums(triples, group_size, lag_count):
    tok_rows, channels = triples[0][0].shape
    flat = [block for triple in triples for block in triple]
    chunks = channels // LANES
    per_chunk = LANES // group_size
    spec = pl.BlockSpec((tok_rows, LANES), lambda i: (0, i))
    out = pl.pallas_call(
        lambda *refs: pair_kernel(group_size, lag_count, *refs),
        grid=(chunks,),
        in_specs=[spec] * len(flat),
        out_specs=pl.BlockSpec((1, per_chunk, lag_count), lambda i: (i, 0, 0)),
        out_shape=jax.ShapeDtypeStruct((chunks, per_chunk, lag_count), jnp.float32),
        name="pair_sums",
        cost_estimate=pl.CostEstimate(flops=12_000_000_000, bytes_accessed=2_500_000, transcendentals=0),
    )(*flat)
    return out.reshape(chunks * per_chunk, lag_count)


def convolve_kernel(group_size, spans, *refs):
    matrix_ref, gate_ref, grad_ref = refs[:3]
    value_refs = refs[3 : 3 + spans]
    mixed_refs = refs[3 + spans : 3 + 2 * spans]
    output_ref, grad_gate_ref, grad_conv_ref = refs[3 + 2 * spans :]
    per_chunk, tok_rows, width = matrix_ref.shape
    flip = exchange_matrix(tok_rows)
    right = jnp.concatenate(
        [
            jnp.concatenate([value_refs[m][...], mixed_refs[m][...]], axis=1)
            for m in range(spans)
        ],
        axis=0,
    )
    left = matrix_ref[...].reshape(per_chunk * tok_rows, width)
    product = jnp.dot(left, right, preferred_element_type=jnp.float32)
    owner = lane_group((tok_rows, 2 * LANES), group_size) % per_chunk
    chosen = product[:tok_rows]
    for g in range(1, per_chunk):
        chosen = jnp.where(owner == g, product[g * tok_rows : (g + 1) * tok_rows], chosen)
    convolved = chosen[:, :LANES]
    gate = jnp.dot(flip, gate_ref[...], preferred_element_type=jnp.float32)
    grad = jnp.dot(flip, grad_ref[...], preferred_element_type=jnp.float32)
    output_ref[...] = reversed_rows(flip, (gate * convolved).astype(jnp.bfloat16))
    grad_gate_ref[...] = reversed_rows(flip, (grad * convolved).astype(jnp.bfloat16))
    grad_conv_ref[...] = chosen[:, LANES:].astype(jnp.bfloat16)


def convolve(matrix, gate_rows, grad_rows, values, mixed, group_size):
    groups, tok_rows, width = matrix.shape
    channels = gate_rows.shape[1]
    chunks = channels // LANES
    per_chunk = LANES // group_size
    spec = pl.BlockSpec((tok_rows, LANES), lambda i: (0, i))
    shape = jax.ShapeDtypeStruct((tok_rows, channels), jnp.bfloat16)
    spans = len(values)
    return pl.pallas_call(
        lambda *refs: convolve_kernel(group_size, spans, *refs),
        grid=(chunks,),
        in_specs=[pl.BlockSpec((per_chunk, tok_rows, width), lambda i: (i, 0, 0))]
        + [spec] * (2 + 2 * spans),
        out_specs=[spec] * 3,
        out_shape=[shape] * 3,
        name="convolve",
        cost_estimate=pl.CostEstimate(flops=12_000_000_000, bytes_accessed=10_500_000, transcendentals=0),
    )(matrix, gate_rows, grad_rows, *values, *mixed)


def owner_sums(partial_value):
    groups, lag_count = partial_value.shape
    members = lax.axis_size("dp") * lax.axis_size("ctx")
    own = lag_count // members
    pieces = partial_value.reshape(groups, members, own).transpose(1, 0, 2)
    pieces = pieces.reshape(members, groups * own)
    met = lax.all_to_all(pieces, ("dp", "ctx"), 0, 0, tiled=True)
    return jnp.sum(met, axis=0).reshape(groups, own)


def shards(gate_input, conv_input, grad_output, kernel):
    tok_rows = gate_input.shape[1]
    channels = gate_input.shape[2]
    groups = kernel.shape[0]
    group_size = channels // groups
    lag_count = kernel.shape[1]
    lag_blocks = lag_count // tok_rows
    blocks = lax.axis_size("ctx")
    gate_rows, value_rows, grad_rows = gate_input[0], conv_input[0], grad_output[0]

    mixed_rows, reversed_values = prepare(gate_rows, value_rows, grad_rows)
    values, mixed = [reversed_values], [mixed_rows]
    for _ in range(lag_blocks):
        values.append(passed_along(values[-1], "ctx", 1))
        mixed.append(passed_along(mixed[-1], "ctx", -1))
    matrix = toeplitz(kernel, tok_rows)
    triples = [(mixed[k], values[k], values[k + 1]) for k in range(lag_blocks // 2 + 1)]
    partial_value = pair_sums(triples, group_size, lag_count)
    summed = owner_sums(partial_value)
    output, grad_gate, grad_conv = convolve(
        matrix, gate_rows, grad_rows, values, mixed, group_size
    )
    grad_kernel = summed / math.sqrt(lax.axis_size("dp") * tok_rows * blocks)
    return (output[None], grad_gate[None], grad_conv[None], grad_kernel)


def solution(mesh):
    return jax.shard_map(
        shards,
        mesh=mesh,
        in_specs=(P("dp", "ctx", "ch"), P("dp", "ctx", "ch"), P("dp", "ctx", "ch"), P("ch", None)),
        out_specs=(
            P("dp", "ctx", "ch"),
            P("dp", "ctx", "ch"),
            P("dp", "ctx", "ch"),
            P("ch", ("dp", "ctx")),
        ),
        check_vma=False,
    )
```

```python
import math

import jax
import jax.numpy as jnp
from jax import lax
from jax.experimental import pallas as pl
from jax.experimental.pallas import tpu as pltpu
from jax.sharding import PartitionSpec as P

LANES = 128
SCOPED = 16 * 1024 * 1024


def exchange_matrix(size):
    rows = lax.broadcasted_iota(jnp.int32, (size, size), 0)
    cols = lax.broadcasted_iota(jnp.int32, (size, size), 1)
    return jnp.where(rows + cols == size - 1, 1.0, 0.0).astype(jnp.bfloat16)


def reversed_rows(flip, block):
    return jnp.dot(flip, block, preferred_element_type=jnp.float32).astype(jnp.bfloat16)


def prepare_kernel(gate_ref, value_ref, grad_ref, mixed_ref, reversed_ref):
    flip = exchange_matrix(value_ref.shape[0])
    mixed_ref[...] = (
        gate_ref[...].astype(jnp.float32) * grad_ref[...].astype(jnp.float32)
    ).astype(jnp.bfloat16)
    reversed_ref[...] = reversed_rows(flip, value_ref[...])


def prepare(gate_rows, value_rows, grad_rows):
    shape = jax.ShapeDtypeStruct(gate_rows.shape, jnp.bfloat16)
    return pl.pallas_call(
        prepare_kernel,
        out_shape=(shape, shape),
        name="prepare",
        compiler_params=pltpu.CompilerParams(vmem_limit_bytes=SCOPED),
        cost_estimate=pl.CostEstimate(flops=40_000_000, bytes_accessed=1_400_000, transcendentals=0),
    )(gate_rows, value_rows, grad_rows)


def toeplitz_kernel(taps_ref, matrix_ref):
    groups, tok_rows, width = matrix_ref.shape
    taps = taps_ref[...].astype(jnp.float32)
    padded = jnp.concatenate([taps, jnp.zeros((groups, width - taps.shape[1]), jnp.float32)], axis=1)
    for g in range(groups):
        spread = jnp.broadcast_to(padded[g : g + 1, :], (tok_rows, width))
        sheared = pltpu.roll(spread, 0, 1, stride=1, stride_axis=0)
        matrix_ref[g] = sheared.astype(jnp.bfloat16)


def toeplitz(taps, tok_rows):
    groups, lag_count = taps.shape
    step = 8
    width = lag_count + tok_rows
    return pl.pallas_call(
        toeplitz_kernel,
        grid=(groups // step,),
        in_specs=[pl.BlockSpec((step, lag_count), lambda i: (i, 0))],
        out_specs=pl.BlockSpec((step, tok_rows, width), lambda i: (i, 0, 0)),
        out_shape=jax.ShapeDtypeStruct((groups, tok_rows, width), jnp.bfloat16),
        name="toeplitz",
        cost_estimate=pl.CostEstimate(flops=12_000_000_000, bytes_accessed=6_400_000, transcendentals=0),
    )(taps)


def lane_group(shape, group_size):
    return lax.broadcasted_iota(jnp.int32, shape, len(shape) - 1) // group_size


def parity_select(parity, even, odd):
    return jnp.where(parity == 0, even, odd)


def lag_window(left_block, right_block, owner, per_chunk):
    tok_rows = left_block.shape[0]
    left = jnp.concatenate(
        [jnp.where(owner == g, left_block, jnp.zeros_like(left_block)) for g in range(per_chunk)],
        axis=0,
    )
    paired = lax.dot_general(
        left, right_block, (((1,), (1,)), ((), ())), preferred_element_type=jnp.float32
    )
    halves = []
    for g in range(per_chunk):
        mine = paired[g * tok_rows : (g + 1) * tok_rows]
        wide = jnp.concatenate([mine, jnp.zeros_like(mine)], axis=1)
        sheared = pltpu.roll(wide, 1, 1, stride=1, stride_axis=0)
        total = jnp.sum(sheared, axis=0, keepdims=True)
        halves.append((total[:, :tok_rows], total[:, tok_rows:]))
    return halves


def gathered_windows(windows, lag_blocks, per_chunk, tok_rows):
    rows = []
    for g in range(per_chunk):
        pieces = []
        for piece in range(lag_blocks):
            held = jnp.zeros((1, tok_rows), jnp.float32)
            if piece in windows:
                held = held + windows[piece][g][1]
            if piece + 1 in windows:
                held = held + windows[piece + 1][g][0]
            pieces.append(held)
        rows.append(jnp.concatenate(pieces, axis=1))
    return jnp.concatenate(rows, axis=0)


def near_kernel(group_size, parity_ref, mixed, mixed_swap, mixed_one, value, value_one, out_ref):
    tok_rows = mixed.shape[0]
    per_chunk, lag_count = out_ref.shape[1:]
    owner = lane_group((tok_rows, LANES), group_size)
    parity = parity_ref[0]
    second = parity_select(parity, value[...], value_one[...])
    windows = {
        0: lag_window(mixed[...], value[...], owner, per_chunk),
        2: lag_window(mixed[...], value_one[...], owner, per_chunk),
        4: lag_window(mixed_one[...], value_one[...], owner, per_chunk),
        1: lag_window(mixed_swap[...], second, owner, per_chunk),
    }
    out_ref[0] = gathered_windows(windows, lag_count // tok_rows, per_chunk, tok_rows)


def far_kernel(
    group_size, parity_ref, near_ref, mixed_swap, mixed_swap_one, value_one, value_two, out_ref, held_ref
):
    step = pl.program_id(0)
    tok_rows = mixed_swap.shape[0]
    chunks, per_chunk, lag_count = held_ref.shape
    owner = lane_group((tok_rows, LANES), group_size)
    parity = parity_ref[0]
    third = parity_select(parity, value_one[...], value_two[...])
    fifth = parity_select(parity, mixed_swap[...], mixed_swap_one[...])
    windows = {
        3: lag_window(mixed_swap[...], third, owner, per_chunk),
        5: lag_window(fifth, value_two[...], owner, per_chunk),
    }
    held_ref[step] = near_ref[0] + gathered_windows(
        windows, lag_count // tok_rows, per_chunk, tok_rows
    )

    @pl.when(step == chunks - 1)
    def _():
        groups = chunks * per_chunk
        members = out_ref.shape[0]
        own = lag_count // members
        sums = jnp.concatenate([held_ref[i] for i in range(chunks)], axis=0)
        high = sums.astype(jnp.bfloat16)
        rest = sums - high.astype(jnp.float32)
        middle = rest.astype(jnp.bfloat16)
        low = (rest - middle.astype(jnp.float32)).astype(jnp.bfloat16)
        lags = lax.broadcasted_iota(jnp.int32, (lag_count, lag_count), 0)
        cols = lax.broadcasted_iota(jnp.int32, (lag_count, lag_count), 1)
        picks = jnp.where(lags == own * (cols % members) + cols // members, 1.0, 0.0)
        split = jnp.dot(
            jnp.concatenate([high, middle, low], axis=0),
            picks.astype(jnp.bfloat16),
            preferred_element_type=jnp.float32,
        )
        moved = split[:groups] + split[groups : 2 * groups] + split[2 * groups :]
        out_ref[:, 0, :] = jnp.concatenate(
            [moved[:, r * members : (r + 1) * members].T for r in range(own)], axis=1
        )


def pair_sums(parity, mixed, values, group_size, lag_count, members):
    tok_rows, channels = values["own"].shape
    chunks = channels // LANES
    per_chunk = LANES // group_size
    groups = chunks * per_chunk
    own = lag_count // members
    spec = pl.BlockSpec((tok_rows, LANES), lambda i: (0, i))
    scalar = pl.BlockSpec(memory_space=pltpu.SMEM)
    part = pl.BlockSpec((1, per_chunk, lag_count), lambda i: (i, 0, 0))
    near = pl.pallas_call(
        lambda *refs: near_kernel(group_size, *refs),
        grid=(chunks,),
        in_specs=[scalar] + [spec] * 5,
        out_specs=part,
        out_shape=jax.ShapeDtypeStruct((chunks, per_chunk, lag_count), jnp.float32),
        name="pair_near",
        compiler_params=pltpu.CompilerParams(vmem_limit_bytes=SCOPED),
        cost_estimate=pl.CostEstimate(flops=8_000_000_000, bytes_accessed=1_500_000, transcendentals=0),
    )(parity, mixed["own"], mixed["swap"], mixed["one"], values["own"], values["one"])
    return pl.pallas_call(
        lambda *refs: far_kernel(group_size, *refs),
        grid=(chunks,),
        in_specs=[scalar, part] + [spec] * 4,
        out_specs=pl.BlockSpec((members, 1, groups * own), lambda i: (0, 0, 0)),
        out_shape=jax.ShapeDtypeStruct((members, 1, groups * own), jnp.float32),
        scratch_shapes=[pltpu.VMEM((chunks, per_chunk, lag_count), jnp.float32)],
        name="pair_far",
        compiler_params=pltpu.CompilerParams(vmem_limit_bytes=SCOPED),
        cost_estimate=pl.CostEstimate(flops=4_000_000_000, bytes_accessed=1_500_000, transcendentals=0),
    )(parity, near, mixed["swap"], mixed["swap_one"], values["one"], values["two"])


NAMES = ("own", "swap", "one", "swap_one", "two", "swap_two", "three")


def convolve_kernel(group_size, *refs):
    parity_ref, matrix_ref, gate_ref, grad_ref = refs[:4]
    value = {name: ref[...] for name, ref in zip(NAMES, refs[4:11])}
    mixed = {name: ref[...] for name, ref in zip(NAMES, refs[11:18])}
    output_ref, grad_gate_ref, grad_conv_ref = refs[18:]
    per_chunk, tok_rows, width = matrix_ref.shape
    parity = parity_ref[0]
    flip = exchange_matrix(tok_rows)
    values = [
        value["own"],
        parity_select(parity, value["swap_one"], value["swap"]),
        value["one"],
        parity_select(parity, value["swap_two"], value["swap_one"]),
        value["two"],
        parity_select(parity, value["three"], value["swap_two"]),
    ]
    mixes = [
        mixed["own"],
        parity_select(parity, mixed["swap"], mixed["swap_one"]),
        mixed["one"],
        parity_select(parity, mixed["swap_one"], mixed["swap_two"]),
        mixed["two"],
        parity_select(parity, mixed["swap_two"], mixed["three"]),
    ]
    right = jnp.concatenate(
        [jnp.concatenate([v, m], axis=1) for v, m in zip(values, mixes)], axis=0
    )
    left = matrix_ref[...].reshape(per_chunk * tok_rows, width)
    product = jnp.dot(left, right, preferred_element_type=jnp.float32)
    owner = lane_group((tok_rows, 2 * LANES), group_size) % per_chunk
    chosen = product[:tok_rows]
    for g in range(1, per_chunk):
        chosen = jnp.where(owner == g, product[g * tok_rows : (g + 1) * tok_rows], chosen)
    convolved = chosen[:, :LANES]
    gate = jnp.dot(flip, gate_ref[...], preferred_element_type=jnp.float32)
    grad = jnp.dot(flip, grad_ref[...], preferred_element_type=jnp.float32)
    output_ref[...] = reversed_rows(flip, (gate * convolved).astype(jnp.bfloat16))
    grad_gate_ref[...] = reversed_rows(flip, (grad * convolved).astype(jnp.bfloat16))
    grad_conv_ref[...] = chosen[:, LANES:].astype(jnp.bfloat16)


def convolve(parity, matrix, gate_rows, grad_rows, values, mixed, group_size):
    groups, tok_rows, width = matrix.shape
    channels = gate_rows.shape[1]
    chunks = channels // LANES
    per_chunk = LANES // group_size
    spec = pl.BlockSpec((tok_rows, LANES), lambda i: (0, i))
    scalar = pl.BlockSpec(memory_space=pltpu.SMEM)
    shape = jax.ShapeDtypeStruct((tok_rows, channels), jnp.bfloat16)
    return pl.pallas_call(
        lambda *refs: convolve_kernel(group_size, *refs),
        grid=(chunks,),
        in_specs=[scalar, pl.BlockSpec((per_chunk, tok_rows, width), lambda i: (i, 0, 0))]
        + [spec] * 16,
        out_specs=[spec] * 3,
        out_shape=[shape] * 3,
        name="convolve",
        compiler_params=pltpu.CompilerParams(vmem_limit_bytes=59 * 1024 * 1024),
        cost_estimate=pl.CostEstimate(flops=12_000_000_000, bytes_accessed=10_500_000, transcendentals=0),
    )(
        parity,
        matrix,
        gate_rows,
        grad_rows,
        *[values[name] for name in NAMES],
        *[mixed[name] for name in NAMES],
    )


def moved(x, by, lands):
    length = lax.axis_size("ctx")
    pairs = [(i, i + by) for i in range(length) if 0 <= i + by < length and lands(i + by)]
    return lax.ppermute(x, "ctx", pairs)


def swapped(x):
    return lax.ppermute(x, "ctx", [(i, i ^ 1) for i in range(lax.axis_size("ctx"))])


def shards(gate_input, conv_input, grad_output, kernel):
    tok_rows = gate_input.shape[1]
    channels = gate_input.shape[2]
    groups = kernel.shape[0]
    group_size = channels // groups
    lag_count = kernel.shape[1]
    blocks = lax.axis_size("ctx")
    members = lax.axis_size("dp") * blocks
    gate_rows, value_rows, grad_rows = gate_input[0], conv_input[0], grad_output[0]
    parity = lax.rem(lax.axis_index("ctx"), 2).reshape(1)
    anyone = lambda i: True
    even = lambda i: i % 2 == 0
    odd = lambda i: i % 2 == 1

    mixed_rows, reversed_values = prepare(gate_rows, value_rows, grad_rows)
    values, mixed = {"own": reversed_values}, {"own": mixed_rows}
    values["one"] = moved(values["own"], 2, anyone)
    mixed["one"] = moved(mixed["own"], -2, anyone)
    mixed["swap"] = swapped(mixed["own"])
    values["swap"] = swapped(values["own"])
    matrix = toeplitz(kernel, tok_rows)
    values["two"] = moved(values["one"], 2, anyone)
    mixed["two"] = moved(mixed["one"], -2, anyone)
    mixed["swap_one"] = swapped(mixed["one"])
    values["swap_one"] = swapped(values["one"])
    pieces = pair_sums(parity, mixed, values, group_size, lag_count, members)
    values["three"] = moved(values["two"], 1, even)
    mixed["three"] = moved(mixed["two"], -1, odd)
    values["swap_two"] = swapped(values["two"])
    mixed["swap_two"] = swapped(mixed["two"])
    met = lax.all_to_all(pieces, ("dp", "ctx"), 0, 0, tiled=True)
    output, grad_gate, grad_conv = convolve(
        parity, matrix, gate_rows, grad_rows, values, mixed, group_size
    )
    summed = jnp.sum(met, axis=(0, 1)).reshape(lag_count // members, groups).T
    grad_kernel = summed / math.sqrt(lax.axis_size("dp") * tok_rows * blocks)
    return (output[None], grad_gate[None], grad_conv[None], grad_kernel)


def solution(mesh):
    return jax.shard_map(
        shards,
        mesh=mesh,
        in_specs=(P("dp", "ctx", "ch"), P("dp", "ctx", "ch"), P("dp", "ctx", "ch"), P("ch", None)),
        out_specs=(
            P("dp", "ctx", "ch"),
            P("dp", "ctx", "ch"),
            P("dp", "ctx", "ch"),
            P("ch", ("dp", "ctx")),
        ),
        check_vma=False,
    )
```

```python
import math

import jax
import jax.numpy as jnp
from jax import lax
from jax.experimental import pallas as pl
from jax.experimental.pallas import tpu as pltpu
from jax.sharding import PartitionSpec as P

LANES = 128
SCOPED = 16 * 1024 * 1024
CROSS = jnp.float32


def exchange_matrix(size):
    rows = lax.broadcasted_iota(jnp.int32, (size, size), 0)
    cols = lax.broadcasted_iota(jnp.int32, (size, size), 1)
    return jnp.where(rows + cols == size - 1, 1.0, 0.0).astype(jnp.bfloat16)


def reversed_rows(flip, block):
    return jnp.dot(flip, block, preferred_element_type=jnp.float32).astype(jnp.bfloat16)


def prepare_kernel(gate_ref, value_ref, grad_ref, mixed_ref, reversed_ref):
    flip = exchange_matrix(value_ref.shape[0])
    mixed_ref[...] = (
        gate_ref[...].astype(jnp.float32) * grad_ref[...].astype(jnp.float32)
    ).astype(jnp.bfloat16)
    reversed_ref[...] = reversed_rows(flip, value_ref[...])


def prepare(gate_rows, value_rows, grad_rows):
    shape = jax.ShapeDtypeStruct(gate_rows.shape, jnp.bfloat16)
    return pl.pallas_call(
        prepare_kernel,
        out_shape=(shape, shape),
        name="prepare",
        cost_estimate=pl.CostEstimate(flops=40_000_000, bytes_accessed=1_400_000, transcendentals=0),
    )(gate_rows, value_rows, grad_rows)


def toeplitz_kernel(taps_ref, even_ref, odd_ref):
    groups, tok_rows, width = even_ref.shape
    taps = taps_ref[...].astype(jnp.float32)
    padded = jnp.concatenate(
        [taps, jnp.zeros((groups, 2 * width - taps.shape[1]), jnp.float32)], axis=1
    )
    for g in range(groups):
        spread = jnp.broadcast_to(padded[g : g + 1, :], (tok_rows, 2 * width))
        sheared = pltpu.roll(spread, 0, 1, stride=1, stride_axis=0).astype(jnp.bfloat16)
        for at in range(0, width, tok_rows):
            even_ref[g, :, at : at + tok_rows] = sheared[:, 2 * at : 2 * at + tok_rows]
            odd_ref[g, :, at : at + tok_rows] = sheared[:, 2 * at + tok_rows : 2 * at + 2 * tok_rows]


def toeplitz(taps, tok_rows):
    groups, lag_count = taps.shape
    step = 8
    width = (lag_count + tok_rows) // 2
    spec = pl.BlockSpec((step, tok_rows, width), lambda i: (i, 0, 0))
    shape = jax.ShapeDtypeStruct((groups, tok_rows, width), jnp.bfloat16)
    return pl.pallas_call(
        toeplitz_kernel,
        grid=(groups // step,),
        in_specs=[pl.BlockSpec((step, lag_count), lambda i: (i, 0))],
        out_specs=[spec, spec],
        out_shape=[shape, shape],
        name="toeplitz",
        cost_estimate=pl.CostEstimate(flops=8_000_000_000, bytes_accessed=6_400_000, transcendentals=0),
    )(taps)


def lane_group(shape, group_size):
    return lax.broadcasted_iota(jnp.int32, shape, len(shape) - 1) // group_size


def parity_select(parity, even, odd):
    return jnp.where(parity == 0, even, odd)


def lag_window(left_block, right_block, owner, per_chunk):
    tok_rows = left_block.shape[0]
    left = jnp.concatenate(
        [jnp.where(owner == g, left_block, jnp.zeros_like(left_block)) for g in range(per_chunk)],
        axis=0,
    )
    paired = lax.dot_general(
        left, right_block, (((1,), (1,)), ((), ())), preferred_element_type=jnp.float32
    )
    halves = []
    for g in range(per_chunk):
        mine = paired[g * tok_rows : (g + 1) * tok_rows]
        wide = jnp.concatenate([mine, jnp.zeros_like(mine)], axis=1)
        sheared = pltpu.roll(wide, 1, 1, stride=1, stride_axis=0)
        total = jnp.sum(sheared, axis=0, keepdims=True)
        halves.append((total[:, :tok_rows], total[:, tok_rows:]))
    return halves


def gathered_windows(windows, lag_blocks, per_chunk, tok_rows):
    rows = []
    for g in range(per_chunk):
        pieces = []
        for piece in range(lag_blocks):
            held = jnp.zeros((1, tok_rows), jnp.float32)
            if piece in windows:
                held = held + windows[piece][g][1]
            if piece + 1 in windows:
                held = held + windows[piece + 1][g][0]
            pieces.append(held)
        rows.append(jnp.concatenate(pieces, axis=1))
    return jnp.concatenate(rows, axis=0)


def near_kernel(group_size, parity_ref, mixed, mixed_swap, mixed_one, value, value_one, out_ref):
    tok_rows = mixed.shape[0]
    per_chunk, lag_count = out_ref.shape[1:]
    owner = lane_group((tok_rows, LANES), group_size)
    parity = parity_ref[0]
    second = parity_select(parity, value[...], value_one[...])
    windows = {
        0: lag_window(mixed[...], value[...], owner, per_chunk),
        2: lag_window(mixed[...], value_one[...], owner, per_chunk),
        4: lag_window(mixed_one[...], value_one[...], owner, per_chunk),
        1: lag_window(mixed_swap[...], second, owner, per_chunk),
    }
    out_ref[0] = gathered_windows(windows, lag_count // tok_rows, per_chunk, tok_rows)


def far_kernel(
    group_size, parity_ref, near_ref, mixed_swap, value_one, value_two, value_three, out_ref, held_ref, turned_ref
):
    step = pl.program_id(0)
    tok_rows = mixed_swap.shape[0]
    chunks, per_chunk, lag_count = held_ref.shape
    owner = lane_group((tok_rows, LANES), group_size)
    parity = parity_ref[0]
    third = parity_select(parity, value_one[...], value_two[...])
    fifth = parity_select(parity, value_two[...], value_three[...])
    windows = {
        3: lag_window(mixed_swap[...], third, owner, per_chunk),
        5: lag_window(mixed_swap[...], fifth, owner, per_chunk),
    }
    held_ref[step] = near_ref[0] + gathered_windows(
        windows, lag_count // tok_rows, per_chunk, tok_rows
    )

    @pl.when(step == chunks - 1)
    def _():
        groups = chunks * per_chunk
        members = out_ref.shape[0]
        own = lag_count // members
        sums = jnp.concatenate([held_ref[i] for i in range(chunks)], axis=0)
        filler = jnp.zeros((LANES - groups, LANES), jnp.float32)
        for at in range(0, lag_count, LANES):
            square = jnp.concatenate([sums[:, at : at + LANES], filler], axis=0)
            turned_ref[at : at + LANES, :] = square.T
        out_ref[:, 0, :] = jnp.concatenate(
            [turned_ref[pl.ds(r, members, stride=own), :][:, :groups] for r in range(own)], axis=1
        )


def pair_sums(parity, mixed, values, group_size, lag_count, members):
    tok_rows, channels = values["own"].shape
    chunks = channels // LANES
    per_chunk = LANES // group_size
    groups = chunks * per_chunk
    own = lag_count // members
    spec = pl.BlockSpec((tok_rows, LANES), lambda i: (0, i))
    scalar = pl.BlockSpec(memory_space=pltpu.SMEM)
    part = pl.BlockSpec((1, per_chunk, lag_count), lambda i: (i, 0, 0))
    near = pl.pallas_call(
        lambda *refs: near_kernel(group_size, *refs),
        grid=(chunks,),
        in_specs=[scalar] + [spec] * 5,
        out_specs=part,
        out_shape=jax.ShapeDtypeStruct((chunks, per_chunk, lag_count), jnp.float32),
        name="pair_near",
        compiler_params=pltpu.CompilerParams(vmem_limit_bytes=SCOPED),
        cost_estimate=pl.CostEstimate(flops=8_000_000_000, bytes_accessed=1_500_000, transcendentals=0),
    )(parity, mixed["own"], mixed["swap"], mixed["one"], values["own"], values["one"])
    return pl.pallas_call(
        lambda *refs: far_kernel(group_size, *refs),
        grid=(chunks,),
        in_specs=[scalar, part] + [spec] * 4,
        out_specs=pl.BlockSpec((members, 1, groups * own), lambda i: (0, 0, 0)),
        out_shape=jax.ShapeDtypeStruct((members, 1, groups * own), jnp.float32),
        scratch_shapes=[
            pltpu.VMEM((chunks, per_chunk, lag_count), jnp.float32),
            pltpu.VMEM((lag_count, LANES), jnp.float32),
        ],
        name="pair_far",
        compiler_params=pltpu.CompilerParams(vmem_limit_bytes=SCOPED),
        cost_estimate=pl.CostEstimate(flops=4_000_000_000, bytes_accessed=1_500_000, transcendentals=0),
    )(parity, near, mixed["swap"], values["one"], values["two"], values["three"])


def group_product(matrix_ref, values, mixes, group_size):
    per_chunk, tok_rows, width = matrix_ref.shape
    right = jnp.concatenate(
        [jnp.concatenate([v, m], axis=1) for v, m in zip(values, mixes)], axis=0
    )
    left = matrix_ref[...].reshape(per_chunk * tok_rows, width)
    product = jnp.dot(left, right, preferred_element_type=jnp.float32)
    owner = lane_group((tok_rows, 2 * LANES), group_size) % per_chunk
    chosen = product[:tok_rows]
    for g in range(1, per_chunk):
        chosen = jnp.where(owner == g, product[g * tok_rows : (g + 1) * tok_rows], chosen)
    return chosen[:, :LANES], chosen[:, LANES:]


def own_kernel(group_size, *refs):
    matrix_ref = refs[0]
    convolved, grads = group_product(
        matrix_ref, [r[...] for r in refs[1:4]], [r[...] for r in refs[4:7]], group_size
    )
    out_ref = refs[7]
    out_ref[0], out_ref[1] = convolved, grads


def cross_kernel(group_size, *refs):
    parity = refs[0][0]
    value, mixed = [r[...] for r in refs[2:6]], [r[...] for r in refs[6:10]]
    values = [parity_select(parity, value[m], value[m + 1]) for m in range(3)]
    mixes = [parity_select(parity, mixed[m + 1], mixed[m]) for m in range(3)]
    convolved, grads = group_product(refs[1], values, mixes, group_size)
    out_ref = refs[10]
    out_ref[0], out_ref[1] = convolved.astype(out_ref.dtype), grads.astype(out_ref.dtype)


def finish_kernel(gate_ref, grad_ref, own_ref, met_ref, output_ref, grad_gate_ref, grad_conv_ref):
    flip = exchange_matrix(gate_ref.shape[0])
    convolved = own_ref[0] + met_ref[0].astype(jnp.float32)
    gate = jnp.dot(flip, gate_ref[...], preferred_element_type=jnp.float32)
    grad = jnp.dot(flip, grad_ref[...], preferred_element_type=jnp.float32)
    output_ref[...] = reversed_rows(flip, (gate * convolved).astype(jnp.bfloat16))
    grad_gate_ref[...] = reversed_rows(flip, (grad * convolved).astype(jnp.bfloat16))
    grad_conv_ref[...] = (own_ref[1] + met_ref[1].astype(jnp.float32)).astype(jnp.bfloat16)


def half_convolve(kernel, name, matrix, blocks, group_size, kind, grant, leading=()):
    groups, tok_rows, width = matrix.shape
    channels = blocks[0].shape[1]
    per_chunk = LANES // group_size
    spec = pl.BlockSpec((tok_rows, LANES), lambda i: (0, i))
    return pl.pallas_call(
        lambda *refs: kernel(group_size, *refs),
        grid=(channels // LANES,),
        in_specs=[pl.BlockSpec(memory_space=pltpu.SMEM)] * len(leading)
        + [pl.BlockSpec((per_chunk, tok_rows, width), lambda i: (i, 0, 0))]
        + [spec] * len(blocks),
        out_specs=pl.BlockSpec((2, tok_rows, LANES), lambda i: (0, 0, i)),
        out_shape=jax.ShapeDtypeStruct((2, tok_rows, channels), kind),
        name=name,
        compiler_params=pltpu.CompilerParams(vmem_limit_bytes=grant),
        cost_estimate=pl.CostEstimate(flops=5_000_000_000, bytes_accessed=5_500_000, transcendentals=0),
    )(*leading, matrix, *blocks)


def finish(gate_rows, grad_rows, own_part, met_part):
    tok_rows, channels = gate_rows.shape
    lanes = 2 * LANES
    spec = pl.BlockSpec((tok_rows, lanes), lambda i: (0, i))
    pair = pl.BlockSpec((2, tok_rows, lanes), lambda i: (0, 0, i))
    shape = jax.ShapeDtypeStruct((tok_rows, channels), jnp.bfloat16)
    return pl.pallas_call(
        finish_kernel,
        grid=(channels // lanes,),
        in_specs=[spec, spec, pair, pair],
        out_specs=[spec] * 3,
        out_shape=[shape] * 3,
        name="finish",
        cost_estimate=pl.CostEstimate(flops=200_000_000, bytes_accessed=3_500_000, transcendentals=0),
    )(gate_rows, grad_rows, own_part, met_part)


def moved(x, by, lands):
    length = lax.axis_size("ctx")
    pairs = [(i, i + by) for i in range(length) if 0 <= i + by < length and lands(i + by)]
    return lax.ppermute(x, "ctx", pairs)


def swapped(x):
    return lax.ppermute(x, "ctx", [(i, i ^ 1) for i in range(lax.axis_size("ctx"))])


def shards(gate_input, conv_input, grad_output, kernel):
    tok_rows = gate_input.shape[1]
    channels = gate_input.shape[2]
    groups = kernel.shape[0]
    group_size = channels // groups
    lag_count = kernel.shape[1]
    blocks = lax.axis_size("ctx")
    members = lax.axis_size("dp") * blocks
    gate_rows, value_rows, grad_rows = gate_input[0], conv_input[0], grad_output[0]
    parity = lax.rem(lax.axis_index("ctx"), 2).reshape(1)
    anyone = lambda i: True
    even = lambda i: i % 2 == 0
    odd = lambda i: i % 2 == 1

    mixed_rows, reversed_values = prepare(gate_rows, value_rows, grad_rows)
    values, mixed = {"own": reversed_values}, {"own": mixed_rows}
    values["one"] = moved(values["own"], 2, anyone)
    mixed["one"] = moved(mixed["own"], -2, anyone)
    mixed["swap"] = swapped(mixed["own"])
    even_matrix, odd_matrix = toeplitz(kernel, tok_rows)
    values["two"] = moved(values["one"], 2, anyone)
    mixed["two"] = moved(mixed["one"], -2, anyone)
    values["three"] = moved(values["two"], 2, odd)
    mixed["three"] = moved(mixed["two"], -2, even)
    pieces = pair_sums(parity, mixed, values, group_size, lag_count, members)
    met = lax.all_to_all(pieces, ("dp", "ctx"), 0, 0, tiled=True)
    near = [t[name] for t in (values, mixed) for name in ("own", "one", "two")]
    every = [t[name] for t in (values, mixed) for name in ("own", "one", "two", "three")]
    own_part = half_convolve(own_kernel, "convolve_own", even_matrix, near, group_size, jnp.float32, None)
    cross_part = half_convolve(
        cross_kernel, "convolve_cross", odd_matrix, every, group_size, CROSS, SCOPED, (parity,)
    )
    output, grad_gate, grad_conv = finish(gate_rows, grad_rows, own_part, swapped(cross_part))
    summed = jnp.sum(met, axis=(0, 1)).reshape(lag_count // members, groups).T
    grad_kernel = summed / math.sqrt(lax.axis_size("dp") * tok_rows * blocks)
    return (output[None], grad_gate[None], grad_conv[None], grad_kernel)


def solution(mesh):
    return jax.shard_map(
        shards,
        mesh=mesh,
        in_specs=(P("dp", "ctx", "ch"), P("dp", "ctx", "ch"), P("dp", "ctx", "ch"), P("ch", None)),
        out_specs=(
            P("dp", "ctx", "ch"),
            P("dp", "ctx", "ch"),
            P("dp", "ctx", "ch"),
            P("ch", ("dp", "ctx")),
        ),
        check_vma=False,
    )
```
